32 devices in a mesh: node: 8 (over z, core), local: 4 (over y, x).
Axes of the slice: x: 2, y: 2, z: 4, core: 2. Of those that a mesh axis runs over, the one named last changes fastest.
Arguments:
- tokens: bfloat16 [256, 3584], P(('node', 'local')), may hold values from -6 to 6
- expert_ids: int32 [256, 4], P(('node', 'local')), may hold values from 0 to 31, as said below
- combine_codes: int32 [256, 4], P(('node', 'local')), may hold values from 1 to 16
- gate_weight: bfloat16 [32, 3584, 1024], P(('node', 'local')), may hold values from -0.09375 to 0.09375
- up_weight: bfloat16 [32, 3584, 1024], P(('node', 'local')), may hold values from -0.09375 to 0.09375
- down_weight: bfloat16 [32, 1024, 3584], P(('node', 'local')), may hold values from -0.1875 to 0.1875
Outputs:
- moe_out: bfloat16 [256, 3584], P(('node', 'local'))
The draws below stay inside these ranges and needn't reach their ends.
Inputs may be any that keep to these rules, and one draw needn't show every extreme that they name: `expert_ids`: expert e belongs to node group e // 4. A token never names two experts of one node group. The 4 ids of each block of 8 rows (the rows of one device) name every node group exactly 4 times. Over all rows r with one value of (r // 8) % 4, no expert is named more than 16 times, and in every node group some expert is named exactly that often.
All inputs are finite; a program needn't handle non-finite values.
Results may differ from the reference program's by a relative error of at most 0.011.
Values may be sent and summed in bfloat16 or wider, within the bound.
A program may use at most 64 MiB of HBM per device.

```python
import jax
import jax.numpy as jnp
from jax import lax

D = 3584
FF = 1024
TOP = 4
EXP_NODE = 4
TOK_DEV = 8
SLICES = 1
H_DEV = 1024
EXPERTS = 32
NODE_ROUTES = 4
EXPERT_CAP = 16
TOKENS = 256
N_NODE = 8
N_LOCAL = 4


def draw_expert_ids(key, part):
    base_key = jax.random.fold_in(key, 11)
    key_nodes, key_hot, key_order = jax.random.split(base_key, 3)
    devices_all = N_NODE * N_LOCAL
    routes_dev = TOK_DEV * TOP
    node_perms = jax.vmap(lambda subkey: jax.random.permutation(subkey, N_NODE))(jax.random.split(key_nodes, devices_all)).astype(jnp.int32)
    route_index = jnp.arange(routes_dev, dtype=jnp.int32)
    target_node = node_perms[:, route_index % N_NODE]
    device_index = jnp.arange(devices_all, dtype=jnp.int32)
    source_node = device_index // N_LOCAL
    source_local = device_index % N_LOCAL
    position = source_node[:, None] * NODE_ROUTES + (route_index // N_NODE)[None, :]
    hottest = jax.random.randint(key_hot, (N_NODE, N_LOCAL), 0, EXP_NODE).astype(jnp.int32)
    others = max(EXP_NODE - 1, 1)
    offset = jnp.where(route_index < EXPERT_CAP, 0, 1 + (route_index - EXPERT_CAP) % others).astype(jnp.int32)
    member_slot = (hottest[:, :, None] + offset[None, None, :]) % EXP_NODE
    shuffles = jax.vmap(lambda subkey: jax.random.permutation(subkey, routes_dev))(jax.random.split(key_order, devices_all)).astype(jnp.int32)
    shuffles = shuffles.reshape(N_NODE, N_LOCAL, routes_dev)
    members = jnp.take_along_axis(member_slot, shuffles, axis=2)
    chosen = members[target_node, source_local[:, None], position]
    expert = target_node * EXP_NODE + chosen
    return expert.reshape(TOK_DEV * devices_all, TOP).astype(jnp.int32)


def place_ends(array, own_key, low, largest):
    place = [jax.random.randint(jax.random.fold_in(own_key, axis), (), 0, length) for axis, length in enumerate(array.shape)]
    main_axis = array.shape.index(max(array.shape))
    next_to = place[:main_axis] + [(place[main_axis] + 1) % array.shape[main_axis]] + place[main_axis + 1:]
    return array.at[tuple(place)].set(low).at[tuple(next_to)].set(largest)


def steps_of(rng, dims, cuts, least, high):
    loudness = 1.0
    for dim, blocks in cuts:
        heights = jax.random.uniform(jax.random.fold_in(jax.random.fold_in(rng, 6), dim), (blocks,), jnp.float32, least / len(cuts), high / len(cuts))
        loudness = loudness * jnp.repeat(jnp.exp(heights), dims[dim] // blocks).reshape((-1,) + (1,) * (len(dims) - 1 - dim))
    return loudness


def scatter_about(stream_key, shape, deviation, bound, cuts=(), held_as=jnp.bfloat16):
    entries = deviation * jax.random.normal(stream_key, shape, jnp.float32)
    if cuts:
        entries = entries * steps_of(stream_key, shape, cuts, -0.22, 0.18)
    return jnp.clip(entries, -bound, bound).astype(held_as)


def setup_inputs(seed: int = 0) -> dict:
    seeds = jax.random.split(jax.random.key(seed), 7)
    return {
        "tokens": scatter_about(seeds[0], (TOKENS, D), 1.0, 6.0, ((0, 32),)),
        "expert_ids": draw_expert_ids(jax.random.fold_in(seeds[6], 71), 0),
        "combine_codes": place_ends(jax.random.randint(seeds[2], (TOKENS, TOP), 1, 17), jax.random.fold_in(seeds[2], 1), 1, 16).astype(jnp.int32),
        "gate_weight": scatter_about(seeds[3], (EXPERTS * SLICES, D, H_DEV), D ** -0.5, 0.09375, ((0, 32),)),
        "up_weight": scatter_about(seeds[4], (EXPERTS * SLICES, D, H_DEV), D ** -0.5, 0.09375, ((0, 32),)),
        "down_weight": scatter_about(seeds[5], (EXPERTS * SLICES, H_DEV, D), FF ** -0.5, 0.1875, ((0, 32),)),
    }


def settle(values):
    return lax.optimization_barrier(values.astype(jnp.bfloat16)).astype(jnp.float32)


def reference(tokens, expert_ids, combine_codes, gate_weight, up_weight, down_weight):
    token_total = tokens.shape[0]
    codes = combine_codes.astype(jnp.float32)
    weights = (codes / jnp.sum(codes, axis=1, keepdims=True)).reshape(-1)
    flat_ids = expert_ids.reshape(-1).astype(jnp.int32)
    order = jnp.argsort(flat_ids, stable=True).astype(jnp.int32)
    counts = jnp.sum((flat_ids[None, :] == jnp.arange(EXPERTS, dtype=jnp.int32)[:, None]).astype(jnp.int32), axis=1)
    starts = (jnp.cumsum(counts) - counts).astype(jnp.int32)
    most = N_LOCAL * EXPERT_CAP
    padded = jnp.concatenate([order, jnp.zeros((most,), jnp.int32)])

    def one_expert(expert, total):
        picked = lax.dynamic_slice_in_dim(padded, starts[expert], most)
        live = jnp.arange(most) < counts[expert]
        owner = jnp.where(live, picked // TOP, token_total).astype(jnp.int32)
        rows = jnp.where(live[:, None], tokens[picked // TOP], 0).astype(jnp.float32)
        first = (expert * SLICES).astype(jnp.int32)
        gate_part = lax.dynamic_slice_in_dim(gate_weight, first, SLICES, 0).astype(jnp.float32)
        up_part = lax.dynamic_slice_in_dim(up_weight, first, SLICES, 0).astype(jnp.float32)
        down_part = lax.dynamic_slice_in_dim(down_weight, first, SLICES, 0).astype(jnp.float32)
        gate = jnp.einsum("rd,sdh->srh", rows, gate_part)
        upper = jnp.einsum("rd,sdh->srh", rows, up_part)
        hidden = settle(jax.nn.silu(gate) * upper)
        partial_out = settle(jnp.einsum("srh,shd->srd", hidden, down_part))
        expert_out = settle(jnp.sum(partial_out, axis=0))
        return total.at[owner].add(weights[picked][:, None] * expert_out)

    total = lax.fori_loop(0, EXPERTS, one_expert, jnp.zeros((token_total + 1, D), jnp.float32))
    return total[:token_total].astype(jnp.bfloat16)
```

```python
import functools

import jax
import jax.numpy as jnp
from jax import lax
from jax.experimental import pallas as pl
from jax.experimental.pallas import tpu as pltpu
from jax.sharding import PartitionSpec as P

MESH = pl.DeviceIdType.MESH
TOP = 4
EXP_NODE = 4
SUB = 8
LAG_IN = 2
LAG_RELAY = 2
LAG_HOME = 3
CHUNKS = 7


def plan(width, per_node):
    chunks = CHUNKS if width % (CHUNKS * 128) == 0 else 1
    chunk = width // chunks
    split = 1
    while per_node * split * 2 <= SUB and chunk % (128 * split * 2) == 0:
        split *= 2
    return chunks, chunk, split


def bf(x):
    return x.astype(jnp.bfloat16)


def dot(a, b):
    return jnp.dot(a, b, preferred_element_type=jnp.float32)


def iota(shape, axis):
    return lax.broadcasted_iota(jnp.int32, shape, axis)


def kernel(
    dims,
    tok_hbm, ids_hbm, codes_hbm, gate_hbm, up_hbm, down_hbm,
    out_ref,
    tok, ids_ref, codes_ref, wg, wu, wd,
    meta_out, meta_in, sel_t, w_hi, w_lo, place, pack,
    msg, arrived, bundle, rows, acc_g, acc_u, hidden, part, back, home_out, home,
    in_sem, w_sem, meta_sem, a_send, a_recv, b_send, b_recv, c_send, c_recv, d_send, d_recv,
):
    nodes, locals_, per_node, cap, chunks, chunk, split = dims
    slices = locals_ // EXP_NODE
    slots = EXP_NODE * cap
    lanes = nodes * SUB
    wide = max(lanes, 128)
    piece = chunk // split
    tokens = tok.shape[1]
    me = lax.axis_index("node")
    my = lax.axis_index("local")

    def small(i, src, dst):
        return pltpu.make_async_copy(src, dst, in_sem.at[i])

    smalls = [small(0, ids_hbm, ids_ref), small(1, codes_hbm, codes_ref)]
    for c in range(chunks):
        smalls.append(small(2 + c, tok_hbm.at[:, pl.ds(c * chunk, chunk)], tok.at[c]))
    for copy in smalls:
        copy.start()

    def w_copy(which, c):
        if which == 2:
            return pltpu.make_async_copy(
                down_hbm.at[0, :, pl.ds(pl.multiple_of(c * chunk, 128), chunk)],
                wd.at[c], w_sem.at[2, c])
        src, dst = ((gate_hbm, wg), (up_hbm, wu))[which]
        return pltpu.make_async_copy(
            src.at[0, pl.ds(pl.multiple_of(c * chunk, 128), chunk), :], dst.at[c],
            w_sem.at[which, c])

    for c in range(chunks):
        w_copy(0, c).start()
        w_copy(1, c).start()
    for c in range(chunks):
        w_copy(2, c).start()

    barrier = pltpu.get_barrier_semaphore()

    def node_peer(d):
        return lax.rem(me + d, nodes)

    def local_peer(d):
        return lax.rem(my + d, locals_)

    @pl.loop(1, nodes)
    def _(d):
        pl.semaphore_signal(barrier, inc=1, device_id=(node_peer(d), my), device_id_type=MESH)

    @pl.loop(1, locals_)
    def _(d):
        pl.semaphore_signal(barrier, inc=1, device_id=(me, local_peer(d)), device_id_type=MESH)

    smalls[0].wait()
    smalls[1].wait()
    ids = ids_ref[...]
    codes = codes_ref[...].astype(jnp.float32)
    code_sum = jnp.sum(codes, axis=1, keepdims=True)
    lane = iota((tokens, 128), 1)
    groups = [lax.div(ids[:, k:k + 1], EXP_NODE) for k in range(TOP)]
    valid = jnp.zeros((tokens, 128), jnp.float32)
    for k in range(TOP):
        valid += jnp.where(lane == groups[k], 1.0, 0.0)
    below = jnp.where(iota((tokens, tokens), 0) > iota((tokens, tokens), 1), 1.0, 0.0)
    rank = dot(below, valid)
    wide_lane = iota((tokens, wide), 1)
    sel = [jnp.zeros((tokens, wide), jnp.float32) for _ in range(split)]
    weight = [jnp.zeros((tokens, wide), jnp.float32) for _ in range(split)]
    member_at = jnp.zeros((tokens, wide), jnp.float32)
    for k in range(TOP):
        rank_k = jnp.sum(jnp.where(lane == groups[k], rank, 0.0), axis=1, keepdims=True)
        spot = groups[k] * SUB + rank_k.astype(jnp.int32)
        member = lax.rem(ids[:, k:k + 1], EXP_NODE).astype(jnp.float32) + 1.0
        share = codes[:, k:k + 1] / code_sum
        for j in range(split):
            hit = wide_lane == spot + j * per_node
            sel[j] = sel[j] + jnp.where(hit, 1.0, 0.0)
            weight[j] = weight[j] + jnp.where(hit, share, 0.0)
            member_at = member_at + jnp.where(hit, member, 0.0)
    for j in range(split):
        sel_t[j] = bf(jnp.transpose(sel[j])[:lanes, :])
        high = bf(weight[j][:, :lanes])
        w_hi[j] = high
        w_lo[j] = bf(weight[j][:, :lanes] - high.astype(jnp.float32))
    member_col = jnp.sum(jnp.transpose(member_at), axis=1, keepdims=True)[:lanes]
    meta_out[...] = jnp.broadcast_to(member_col, (lanes, 128)).astype(jnp.int32).reshape(
        nodes, SUB, 128)
    meta_in[me] = meta_out[me]

    pl.semaphore_wait(barrier, nodes + locals_ - 2)

    def node_send(src, dst, s_sem, r_sem):
        @pl.loop(1, nodes)
        def _(d):
            peer = node_peer(d)
            pltpu.make_async_remote_copy(
                src_ref=src.at[peer], dst_ref=dst.at[me], send_sem=s_sem, recv_sem=r_sem,
                device_id=(peer, my), device_id_type=MESH).start()

    def local_send(src, dst, s_sem, r_sem, per):
        for d in range(1, locals_):
            peer = local_peer(d)
            pltpu.make_async_remote_copy(
                src_ref=src.at[lax.div(peer, per)], dst_ref=dst.at[my], send_sem=s_sem,
                recv_sem=r_sem, device_id=(me, peer), device_id_type=MESH).start()

    def drain(ref, count, sem):
        whole = ref.at[pl.ds(0, count)]
        pltpu.make_async_copy(whole, whole, sem).wait()

    node_send(meta_out, meta_in, meta_sem.at[0], meta_sem.at[1])

    for c in range(chunks):
        smalls[2 + c].wait()

    @pl.loop(0, chunks)
    def _(c):
        total = dot(sel_t[0], tok[c, :, 0:piece])
        for j in range(1, split):
            total += dot(sel_t[j], tok[c, :, j * piece:(j + 1) * piece])
        msg[c] = bf(total.reshape(nodes, SUB, piece))
        arrived[c, me] = msg[c, me]
        node_send(msg.at[c], arrived.at[c], a_send.at[c], a_recv.at[c])

    drain(meta_in, nodes - 1, meta_sem.at[1])
    members = meta_in[...].reshape(lanes, 128)
    lane = iota((lanes, 128), 1)
    row = iota((lanes, 128), 0)
    under = bf(jnp.where(iota((lanes, lanes), 0) > iota((lanes, lanes), 1), 1.0, 0.0))
    for j in range(split):
        inside = lax.div(lax.rem(row, SUB), per_node) == j
        mine = jnp.where(inside, members, 0)
        marks = jnp.where(mine == lane + 1, 1.0, 0.0)
        before = dot(under, bf(marks))
        spot = jnp.sum(before * marks, axis=1, keepdims=True).astype(jnp.int32)
        target = jnp.where(mine > 0, (mine - 1) * cap + spot, -1)
        placed = jnp.where(lane == target, 1.0, 0.0)
        place[j] = bf(placed[:, :slots])
        pack[j] = bf(jnp.transpose(placed)[:slots, :])

    acc_g[...] = jnp.zeros_like(acc_g)
    acc_u[...] = jnp.zeros_like(acc_u)

    @pl.loop(0, chunks + LAG_IN)
    def _(step):
        @pl.when(step < chunks)
        def _():
            c = step
            drain(arrived.at[c], nodes - 1, a_recv.at[c])
            got = arrived[c].reshape(lanes, piece)
            for j in range(split):
                bundle[c, :, :, j * piece:(j + 1) * piece] = bf(
                    dot(pack[j], got).reshape(EXP_NODE, cap, piece))
            rows[c, my] = bundle[c, lax.div(my, slices)]
            local_send(bundle.at[c], rows.at[c], b_send.at[c], b_recv.at[c], slices)

        @pl.when(step >= LAG_IN)
        def _():
            c = step - LAG_IN
            w_copy(0, c).wait()
            w_copy(1, c).wait()
            drain(rows.at[c], locals_ - 1, b_recv.at[c])
            x = rows[c].reshape(locals_ * cap, chunk)
            acc_g[...] += dot(x, wg[c])
            acc_u[...] += dot(x, wu[c])

    gate = acc_g[...]
    hidden[...] = bf(gate / (1.0 + jnp.exp(-gate)) * acc_u[...])

    @pl.loop(0, chunks + LAG_RELAY + LAG_HOME)
    def _(step):
        @pl.when(step < chunks)
        def _():
            c = step
            w_copy(2, c).wait()
            part[c] = bf(dot(hidden[...], wd[c]).reshape(locals_, cap, chunk))
            back[c, my] = part[c, my]
            local_send(part.at[c], back.at[c], c_send.at[c], c_recv.at[c], 1)

        @pl.when((step >= LAG_RELAY) & (step < chunks + LAG_RELAY))
        def _():
            c = step - LAG_RELAY
            drain(back.at[c], locals_ - 1, c_recv.at[c])
            if slices == 1:
                got = back[c].reshape(slots, chunk)
            else:
                got = bf(jnp.sum(
                    back[c].astype(jnp.float32).reshape(EXP_NODE, slices, cap, chunk),
                    axis=1)).reshape(slots, chunk)
            total = dot(place[0], got[:, 0:piece])
            for j in range(1, split):
                total += dot(place[j], got[:, j * piece:(j + 1) * piece])
            home_out[c] = bf(total.reshape(nodes, SUB, piece))
            home[c, me] = home_out[c, me]
            node_send(home_out.at[c], home.at[c], d_send.at[c], d_recv.at[c])

        @pl.when(step >= LAG_RELAY + LAG_HOME)
        def _():
            c = step - LAG_RELAY - LAG_HOME
            drain(home.at[c], nodes - 1, d_recv.at[c])
            got = home[c].reshape(lanes, piece)
            for j in range(split):
                value = dot(w_hi[j], got) + dot(w_lo[j], got)
                at = pl.multiple_of(c * chunk + j * piece, 128)
                out_ref[:, pl.ds(at, piece)] = bf(value)

    drain(meta_out, nodes - 1, meta_sem.at[0])

    @pl.loop(0, chunks)
    def _(c):
        drain(msg.at[c], nodes - 1, a_send.at[c])
        drain(rows.at[c], locals_ - 1, b_send.at[c])
        drain(part.at[c], locals_ - 1, c_send.at[c])
        drain(home_out.at[c], nodes - 1, d_send.at[c])


def body(tokens, expert_ids, combine_codes, gate_weight, up_weight, down_weight):
    nodes = lax.axis_size("node")
    locals_ = lax.axis_size("local")
    count, width = tokens.shape
    hid = gate_weight.shape[2]
    routes = count * TOP
    per_node = routes // nodes
    cap = min(routes, 2 * routes // EXP_NODE)
    chunks, chunk, split = plan(width, per_node)
    piece = chunk // split
    lanes = nodes * SUB
    slots = EXP_NODE * cap
    many = locals_ * cap
    b16, f32, i32 = jnp.bfloat16, jnp.float32, jnp.int32
    dims = (nodes, locals_, per_node, cap, chunks, chunk, split)
    dma = pltpu.SemaphoreType.DMA
    return pl.pallas_call(
        functools.partial(kernel, dims),
        out_shape=jax.ShapeDtypeStruct((count, width), b16),
        in_specs=[pl.BlockSpec(memory_space=pl.ANY)] * 6,
        out_specs=pl.BlockSpec(memory_space=pltpu.VMEM),
        scratch_shapes=[
            pltpu.VMEM((chunks, count, chunk), b16),
            pltpu.VMEM((count, TOP), i32),
            pltpu.VMEM((count, TOP), i32),
            pltpu.VMEM((chunks, chunk, hid), b16),
            pltpu.VMEM((chunks, chunk, hid), b16),
            pltpu.VMEM((chunks, hid, chunk), b16),
            pltpu.VMEM((nodes, SUB, 128), i32),
            pltpu.VMEM((nodes, SUB, 128), i32),
            pltpu.VMEM((split, lanes, count), b16),
            pltpu.VMEM((split, count, lanes), b16),
            pltpu.VMEM((split, count, lanes), b16),
            pltpu.VMEM((split, lanes, slots), b16),
            pltpu.VMEM((split, slots, lanes), b16),
            pltpu.VMEM((chunks, nodes, SUB, piece), b16),
            pltpu.VMEM((chunks, nodes, SUB, piece), b16),
            pltpu.VMEM((chunks, EXP_NODE, cap, chunk), b16),
            pltpu.VMEM((chunks, locals_, cap, chunk), b16),
            pltpu.VMEM((many, hid), f32),
            pltpu.VMEM((many, hid), f32),
            pltpu.VMEM((many, hid), b16),
            pltpu.VMEM((chunks, locals_, cap, chunk), b16),
            pltpu.VMEM((chunks, locals_, cap, chunk), b16),
            pltpu.VMEM((chunks, nodes, SUB, piece), b16),
            pltpu.VMEM((chunks, nodes, SUB, piece), b16),
            dma((2 + chunks,)),
            dma((3, chunks)),
            dma((2,)),
            dma((chunks,)), dma((chunks,)),
            dma((chunks,)), dma((chunks,)),
            dma((chunks,)), dma((chunks,)),
            dma((chunks,)), dma((chunks,)),
        ],
        compiler_params=pltpu.CompilerParams(collective_id=0, has_side_effects=True),
    )(tokens, expert_ids, combine_codes, gate_weight, up_weight, down_weight)


def solution(mesh):
    in_specs = (
        P(("node", "local"), None),
        P(("node", "local"), None),
        P(("node", "local"), None),
        P(("node", "local"), None, None),
        P(("node", "local"), None, None),
        P(("node", "local"), None, None),
    )
    out_specs = P(("node", "local"), None)
    return jax.shard_map(body, mesh=mesh, in_specs=in_specs, out_specs=out_specs, check_vma=False)
```

```python
import functools

import jax
import jax.numpy as jnp
from jax import lax
from jax.experimental import pallas as pl
from jax.experimental.pallas import tpu as pltpu
from jax.sharding import PartitionSpec as P

MESH = pl.DeviceIdType.MESH
TOP = 4
EXP_NODE = 4
SUB = 8
IN_PARTS = (5, 5, 4)
OUT_PARTS = (4, 5, 5)
LAG_IN = 2
LAG_RELAY = 2
LAG_HOME = 2


def cut(units, parts):
    total, seen, edges = sum(parts), 0, [0]
    for part in parts:
        seen += part
        edges.append(units * seen // total)
    return [(a, b - a) for a, b in zip(edges[:-1], edges[1:]) if b > a]


def plan(width, per_node):
    split = 1
    while per_node * split * 2 <= SUB and width % (128 * split * 2) == 0:
        split *= 2
    unit = 128 * split
    scale = lambda spans: [(a * unit, n * unit) for a, n in spans]
    return split, scale(cut(width // unit, IN_PARTS)), scale(cut(width // unit, OUT_PARTS))


def bf(x):
    return x.astype(jnp.bfloat16)


def dot(a, b):
    return jnp.dot(a, b, preferred_element_type=jnp.float32)


def iota(shape, axis):
    return lax.broadcasted_iota(jnp.int32, shape, axis)


def kernel(dims, counts, *refs):
    nodes, locals_, per_node, cap, split, spans_in, spans_out = dims
    refs = iter(refs)
    groups_of = []
    for count in counts:
        taken = [next(refs) for _ in range(max(count, 1))]
        groups_of.append(taken if count else taken[0])
    (tok_hbm, ids_hbm, codes_hbm, gate_hbm, up_hbm, down_hbm, out_ref,
     tok, ids_ref, codes_ref, meta_out, meta_in, sel_t, w_hi, w_lo, place, pack,
     acc_g, acc_u, hidden,
     wg, wu, msg, arrived, bundle, rows,
     wd, part, back, home_out, home,
     in_sem, w_sem, meta_sem, a_send, a_recv, b_send, b_recv,
     c_send, c_recv, d_send, d_recv) = groups_of
    slices = locals_ // EXP_NODE
    slots = EXP_NODE * cap
    lanes = nodes * SUB
    wide = max(lanes, 128)
    tokens = tok.shape[0]
    me = lax.axis_index("node")
    my = lax.axis_index("local")
    n_in, n_out = len(spans_in), len(spans_out)

    smalls = [
        pltpu.make_async_copy(src, dst, in_sem.at[i])
        for i, (src, dst) in enumerate(
            ((ids_hbm, ids_ref), (codes_hbm, codes_ref), (tok_hbm, tok)))
    ]
    for copy in smalls:
        copy.start()

    barrier = pltpu.get_barrier_semaphore()

    def node_peer(d):
        return lax.rem(me + d, nodes)

    def local_peer(d):
        return lax.rem(my + d, locals_)

    @pl.loop(1, nodes)
    def _(d):
        pl.semaphore_signal(barrier, inc=1, device_id=(node_peer(d), my), device_id_type=MESH)

    @pl.loop(1, locals_)
    def _(d):
        pl.semaphore_signal(barrier, inc=1, device_id=(me, local_peer(d)), device_id_type=MESH)

    first = [
        [pltpu.make_async_copy(src.at[0, pl.ds(at, size), :], dst[c], w_sem.at[which, c])
         for which, (src, dst) in enumerate(((gate_hbm, wg), (up_hbm, wu)))]
        for c, (at, size) in enumerate(spans_in)
    ]
    second = [
        pltpu.make_async_copy(down_hbm.at[0, :, pl.ds(at, size)], wd[c], w_sem.at[2, c])
        for c, (at, size) in enumerate(spans_out)
    ]
    for pair in first:
        for copy in pair:
            copy.start()
    for copy in second:
        copy.start()

    smalls[0].wait()
    smalls[1].wait()
    same = iota((tokens, tokens), 0) == iota((tokens, tokens), 1)

    def column(ref, k):
        return jnp.sum(jnp.where(same, ref[k:k + 1, :], 0), axis=1, keepdims=True)

    ids = [column(ids_ref, k) for k in range(TOP)]
    codes = [column(codes_ref, k).astype(jnp.float32) for k in range(TOP)]
    code_sum = sum(codes[1:], codes[0])
    lane = iota((tokens, 128), 1)
    groups = [lax.div(ids[k], EXP_NODE) for k in range(TOP)]
    valid = jnp.zeros((tokens, 128), jnp.float32)
    for k in range(TOP):
        valid += jnp.where(lane == groups[k], 1.0, 0.0)
    below = jnp.where(iota((tokens, tokens), 0) > iota((tokens, tokens), 1), 1.0, 0.0)
    rank = dot(below, valid)
    wide_lane = iota((tokens, wide), 1)
    sel = [jnp.zeros((tokens, wide), jnp.float32) for _ in range(split)]
    weight = [jnp.zeros((tokens, wide), jnp.float32) for _ in range(split)]
    member_at = jnp.zeros((tokens, wide), jnp.float32)
    for k in range(TOP):
        rank_k = jnp.sum(jnp.where(lane == groups[k], rank, 0.0), axis=1, keepdims=True)
        spot = groups[k] * SUB + rank_k.astype(jnp.int32)
        member = lax.rem(ids[k], EXP_NODE).astype(jnp.float32) + 1.0
        share = codes[k] / code_sum
        for j in range(split):
            hit = wide_lane == spot + j * per_node
            sel[j] = sel[j] + jnp.where(hit, 1.0, 0.0)
            weight[j] = weight[j] + jnp.where(hit, share, 0.0)
            member_at = member_at + jnp.where(hit, member, 0.0)
    for j in range(split):
        sel_t[j] = bf(jnp.transpose(sel[j])[:lanes, :])
        high = bf(weight[j][:, :lanes])
        w_hi[j] = high
        w_lo[j] = bf(weight[j][:, :lanes] - high.astype(jnp.float32))
    member_col = jnp.sum(jnp.transpose(member_at), axis=1, keepdims=True)[:lanes]
    meta_out[...] = jnp.broadcast_to(member_col, (lanes, 128)).astype(jnp.int32).reshape(
        nodes, SUB, 128)
    meta_in[me] = meta_out[me]

    def node_send(src, dst, s_sem, r_sem):
        @pl.loop(1, nodes)
        def _(d):
            peer = node_peer(d)
            pltpu.make_async_remote_copy(
                src_ref=src.at[peer], dst_ref=dst.at[me], send_sem=s_sem, recv_sem=r_sem,
                device_id=(peer, my), device_id_type=MESH).start()

    def local_send(src, dst, s_sem, r_sem, per):
        for d in range(1, locals_):
            peer = local_peer(d)
            pltpu.make_async_remote_copy(
                src_ref=src.at[lax.div(peer, per)], dst_ref=dst.at[my], send_sem=s_sem,
                recv_sem=r_sem, device_id=(me, peer), device_id_type=MESH).start()

    def drain(ref, count, sem):
        whole = ref.at[pl.ds(0, count)]
        pltpu.make_async_copy(whole, whole, sem).wait()

    smalls[2].wait()

    def fill_msg(c):
        at, size = spans_in[c]
        piece = size // split
        total = dot(sel_t[0], tok[:, at:at + piece])
        for j in range(1, split):
            total += dot(sel_t[j], tok[:, at + j * piece:at + (j + 1) * piece])
        msg[c][...] = bf(total.reshape(nodes, SUB, piece))
        arrived[c][me] = msg[c][me]

    for c in range(n_in):
        fill_msg(c)
    pl.semaphore_wait(barrier, nodes + locals_ - 2)
    node_send(meta_out, meta_in, meta_sem.at[0], meta_sem.at[1])
    for c in range(n_in):
        node_send(msg[c], arrived[c], a_send.at[c], a_recv.at[c])

    drain(meta_in, nodes - 1, meta_sem.at[1])
    members = meta_in[...].reshape(lanes, 128)
    lane = iota((lanes, 128), 1)
    row = iota((lanes, 128), 0)
    under = bf(jnp.where(iota((lanes, lanes), 0) > iota((lanes, lanes), 1), 1.0, 0.0))
    for j in range(split):
        inside = lax.div(lax.rem(row, SUB), per_node) == j
        mine = jnp.where(inside, members, 0)
        marks = jnp.where(mine == lane + 1, 1.0, 0.0)
        before = dot(under, bf(marks))
        spot = jnp.sum(before * marks, axis=1, keepdims=True).astype(jnp.int32)
        target = jnp.where(mine > 0, (mine - 1) * cap + spot, -1)
        placed = jnp.where(lane == target, 1.0, 0.0)
        place[j] = bf(placed[:, :slots])
        pack[j] = bf(jnp.transpose(placed)[:slots, :])

    def forward(c):
        piece = spans_in[c][1] // split
        drain(arrived[c], nodes - 1, a_recv.at[c])
        got = arrived[c][...].reshape(lanes, piece)
        for j in range(split):
            bundle[c][:, :, j * piece:(j + 1) * piece] = bf(
                dot(pack[j], got).reshape(EXP_NODE, cap, piece))
        rows[c][my] = bundle[c][lax.div(my, slices)]
        local_send(bundle[c], rows[c], b_send.at[c], b_recv.at[c], slices)

    def expand(c):
        first[c][0].wait()
        first[c][1].wait()
        drain(rows[c], locals_ - 1, b_recv.at[c])
        x = rows[c][...].reshape(locals_ * cap, spans_in[c][1])
        if c == 0:
            acc_g[...] = dot(x, wg[c][...])
            acc_u[...] = dot(x, wu[c][...])
        else:
            acc_g[...] += dot(x, wg[c][...])
            acc_u[...] += dot(x, wu[c][...])

    for step in range(n_in + LAG_IN):
        if step < n_in:
            forward(step)
        if step >= LAG_IN:
            expand(step - LAG_IN)

    gate = acc_g[...]
    hidden[...] = bf(gate / (1.0 + jnp.exp(-gate)) * acc_u[...])

    def project(c):
        second[c].wait()
        part[c][...] = bf(dot(hidden[...], wd[c][...]).reshape(locals_, cap, spans_out[c][1]))
        back[c][my] = part[c][my]
        local_send(part[c], back[c], c_send.at[c], c_recv.at[c], 1)

    def relay(c):
        size = spans_out[c][1]
        piece = size // split
        drain(back[c], locals_ - 1, c_recv.at[c])
        if slices == 1:
            got = back[c][...].reshape(slots, size)
        else:
            got = bf(jnp.sum(
                back[c][...].astype(jnp.float32).reshape(EXP_NODE, slices, cap, size),
                axis=1)).reshape(slots, size)
        total = dot(place[0], got[:, 0:piece])
        for j in range(1, split):
            total += dot(place[j], got[:, j * piece:(j + 1) * piece])
        home_out[c][...] = bf(total.reshape(nodes, SUB, piece))
        home[c][me] = home_out[c][me]
        node_send(home_out[c], home[c], d_send.at[c], d_recv.at[c])

    def combine(c):
        at, size = spans_out[c]
        piece = size // split
        drain(home[c], nodes - 1, d_recv.at[c])
        got = home[c][...].reshape(lanes, piece)
        for j in range(split):
            value = dot(w_hi[j], got) + dot(w_lo[j], got)
            out_ref[:, at + j * piece:at + (j + 1) * piece] = bf(value)

    for step in range(n_out + LAG_RELAY + LAG_HOME):
        if step < n_out:
            project(step)
        if LAG_RELAY <= step < n_out + LAG_RELAY:
            relay(step - LAG_RELAY)
        if step >= LAG_RELAY + LAG_HOME:
            combine(step - LAG_RELAY - LAG_HOME)

    drain(meta_out, nodes - 1, meta_sem.at[0])
    for c in range(n_in):
        drain(msg[c], nodes - 1, a_send.at[c])
        drain(rows[c], locals_ - 1, b_send.at[c])
    for c in range(n_out):
        drain(part[c], locals_ - 1, c_send.at[c])
        drain(home_out[c], nodes - 1, d_send.at[c])


def body(tokens, expert_ids, combine_codes, gate_weight, up_weight, down_weight):
    nodes = lax.axis_size("node")
    locals_ = lax.axis_size("local")
    count, width = tokens.shape
    hid = gate_weight.shape[2]
    routes = count * TOP
    per_node = routes // nodes
    cap = min(routes, 2 * routes // EXP_NODE)
    split, spans_in, spans_out = plan(width, per_node)
    lanes = nodes * SUB
    slots = EXP_NODE * cap
    many = locals_ * cap
    b16, f32, i32 = jnp.bfloat16, jnp.float32, jnp.int32
    dims = (nodes, locals_, per_node, cap, split, spans_in, spans_out)
    dma = pltpu.SemaphoreType.DMA
    v = pltpu.VMEM
    most = max(len(spans_in), len(spans_out))
    sizes_in = [n for _, n in spans_in]
    sizes_out = [n for _, n in spans_out]
    scratch = [
        v((count, width), b16), v((TOP, count), i32), v((TOP, count), i32),
        v((nodes, SUB, 128), i32), v((nodes, SUB, 128), i32),
        v((split, lanes, count), b16), v((split, count, lanes), b16),
        v((split, count, lanes), b16),
        v((split, lanes, slots), b16), v((split, slots, lanes), b16),
        v((many, hid), f32), v((many, hid), f32), v((many, hid), b16),
        [v((n, hid), b16) for n in sizes_in],
        [v((n, hid), b16) for n in sizes_in],
        [v((nodes, SUB, n // split), b16) for n in sizes_in],
        [v((nodes, SUB, n // split), b16) for n in sizes_in],
        [v((EXP_NODE, cap, n), b16) for n in sizes_in],
        [v((locals_, cap, n), b16) for n in sizes_in],
        [v((hid, n), b16) for n in sizes_out],
        [v((locals_, cap, n), b16) for n in sizes_out],
        [v((locals_, cap, n), b16) for n in sizes_out],
        [v((nodes, SUB, n // split), b16) for n in sizes_out],
        [v((nodes, SUB, n // split), b16) for n in sizes_out],
        dma((3,)), dma((3, most)), dma((2,)),
    ] + [dma((most,)) for _ in range(8)]
    counts = [0] * 7 + [len(x) if isinstance(x, list) else 0 for x in scratch]
    flat = [y for x in scratch for y in (x if isinstance(x, list) else [x])]
    return pl.pallas_call(
        functools.partial(kernel, dims, counts),
        out_shape=jax.ShapeDtypeStruct((count, width), b16),
        in_specs=[pl.BlockSpec(memory_space=pl.ANY)] * 6,
        out_specs=pl.BlockSpec(memory_space=pltpu.VMEM),
        scratch_shapes=flat,
        compiler_params=pltpu.CompilerParams(collective_id=0, has_side_effects=True),
    )(tokens, expert_ids.T, combine_codes.T, gate_weight, up_weight, down_weight)


def solution(mesh):
    in_specs = (
        P(("node", "local"), None),
        P(("node", "local"), None),
        P(("node", "local"), None),
        P(("node", "local"), None, None),
        P(("node", "local"), None, None),
        P(("node", "local"), None, None),
    )
    out_specs = P(("node", "local"), None)
    return jax.shard_map(body, mesh=mesh, in_specs=in_specs, out_specs=out_specs, check_vma=False)
```

```python
import functools

import jax
import jax.numpy as jnp
from jax import lax
from jax.experimental import pallas as pl
from jax.experimental.pallas import tpu as pltpu
from jax.sharding import PartitionSpec as P

MESH = pl.DeviceIdType.MESH
TOP = 4
EXP_NODE = 4
SUB = 8
IN_PARTS = (5, 4, 3, 2)
OUT_PARTS = (2, 3, 4, 5)
LAG_IN = 3
LAG_RELAY = 3
LAG_HOME = 3


def cut(units, parts):
    total, seen, edges = sum(parts), 0, [0]
    for part in parts:
        seen += part
        edges.append(units * seen // total)
    return [(a, b - a) for a, b in zip(edges[:-1], edges[1:]) if b > a]


def plan(width, per_node):
    split = 1
    while per_node * split * 2 <= SUB and width % (128 * split * 2) == 0:
        split *= 2
    unit = 128 * split
    scale = lambda spans: [(a * unit, n * unit) for a, n in spans]
    return split, scale(cut(width // unit, IN_PARTS)), scale(cut(width // unit, OUT_PARTS))


def bf(x):
    return x.astype(jnp.bfloat16)


def dot(a, b):
    return jnp.dot(a, b, preferred_element_type=jnp.float32)


def iota(shape, axis):
    return lax.broadcasted_iota(jnp.int32, shape, axis)


def kernel(dims, counts, *refs):
    nodes, locals_, per_node, cap, split, spans_in, spans_out = dims
    refs = iter(refs)
    groups_of = []
    for count in counts:
        taken = [next(refs) for _ in range(max(count, 1))]
        groups_of.append(taken if count else taken[0])
    (tok_hbm, ids_hbm, codes_hbm, gate_hbm, up_hbm, down_hbm, out_ref,
     tok, ids_ref, codes_ref, meta_out, meta_in, sel_t, w_hi, w_lo, place, pack,
     acc_g, acc_u, hidden,
     wg, wu, msg, arrived, bundle, rows,
     wd, part, back, home_out, home,
     in_sem, w_sem, meta_sem, a_send, a_recv, b_send, b_recv,
     c_send, c_recv, d_send, d_recv) = groups_of
    slices = locals_ // EXP_NODE
    slots = EXP_NODE * cap
    lanes = nodes * SUB
    wide = max(lanes, 128)
    tokens = tok.shape[0]
    me = lax.axis_index("node")
    my = lax.axis_index("local")
    n_in, n_out = len(spans_in), len(spans_out)

    smalls = [
        pltpu.make_async_copy(src, dst, in_sem.at[i])
        for i, (src, dst) in enumerate(
            ((ids_hbm, ids_ref), (codes_hbm, codes_ref), (tok_hbm, tok)))
    ]
    for copy in smalls:
        copy.start()

    barrier = pltpu.get_barrier_semaphore()

    def node_peer(d):
        return lax.rem(me + d, nodes)

    def local_peer(d):
        return lax.rem(my + d, locals_)

    @pl.loop(1, nodes)
    def _(d):
        pl.semaphore_signal(barrier, inc=1, device_id=(node_peer(d), my), device_id_type=MESH)

    @pl.loop(1, locals_)
    def _(d):
        pl.semaphore_signal(barrier, inc=1, device_id=(me, local_peer(d)), device_id_type=MESH)

    first = [
        [pltpu.make_async_copy(src.at[0, pl.ds(at, size), :], dst[c], w_sem.at[which, c])
         for which, (src, dst) in enumerate(((gate_hbm, wg), (up_hbm, wu)))]
        for c, (at, size) in enumerate(spans_in)
    ]
    second = [
        pltpu.make_async_copy(down_hbm.at[0, :, pl.ds(at, size)], wd[c], w_sem.at[2, c])
        for c, (at, size) in enumerate(spans_out)
    ]
    for pair in first:
        for copy in pair:
            copy.start()
    for copy in second:
        copy.start()

    smalls[0].wait()
    smalls[1].wait()
    same = iota((tokens, tokens), 0) == iota((tokens, tokens), 1)

    def column(ref, k):
        return jnp.sum(jnp.where(same, ref[k:k + 1, :], 0), axis=1, keepdims=True)

    ids = [column(ids_ref, k) for k in range(TOP)]
    codes = [column(codes_ref, k).astype(jnp.float32) for k in range(TOP)]
    code_sum = sum(codes[1:], codes[0])
    lane = iota((tokens, 128), 1)
    groups = [lax.div(ids[k], EXP_NODE) for k in range(TOP)]
    valid = jnp.zeros((tokens, 128), jnp.float32)
    for k in range(TOP):
        valid += jnp.where(lane == groups[k], 1.0, 0.0)
    below = jnp.where(iota((tokens, tokens), 0) > iota((tokens, tokens), 1), 1.0, 0.0)
    rank = dot(below, valid)
    wide_lane = iota((tokens, wide), 1)
    sel = [jnp.zeros((tokens, wide), jnp.float32) for _ in range(split)]
    weight = [jnp.zeros((tokens, wide), jnp.float32) for _ in range(split)]
    member_at = jnp.zeros((tokens, wide), jnp.float32)
    for k in range(TOP):
        rank_k = jnp.sum(jnp.where(lane == groups[k], rank, 0.0), axis=1, keepdims=True)
        spot = groups[k] * SUB + rank_k.astype(jnp.int32)
        member = lax.rem(ids[k], EXP_NODE).astype(jnp.float32) + 1.0
        share = codes[k] / code_sum
        for j in range(split):
            hit = wide_lane == spot + j * per_node
            sel[j] = sel[j] + jnp.where(hit, 1.0, 0.0)
            weight[j] = weight[j] + jnp.where(hit, share, 0.0)
            member_at = member_at + jnp.where(hit, member, 0.0)
    for j in range(split):
        sel_t[j] = bf(jnp.transpose(sel[j])[:lanes, :])
        high = bf(weight[j][:, :lanes])
        w_hi[j] = high
        w_lo[j] = bf(weight[j][:, :lanes] - high.astype(jnp.float32))
    member_col = jnp.sum(jnp.transpose(member_at), axis=1, keepdims=True)[:lanes]
    meta_out[...] = jnp.broadcast_to(member_col, (lanes, 128)).astype(jnp.int32).reshape(
        nodes, SUB, 128)
    meta_in[me] = meta_out[me]

    def node_send(src, dst, s_sem, r_sem):
        @pl.loop(1, nodes)
        def _(d):
            peer = node_peer(d)
            pltpu.make_async_remote_copy(
                src_ref=src.at[peer], dst_ref=dst.at[me], send_sem=s_sem, recv_sem=r_sem,
                device_id=(peer, my), device_id_type=MESH).start()

    def local_send(src, dst, s_sem, r_sem, per):
        for d in range(1, locals_):
            peer = local_peer(d)
            pltpu.make_async_remote_copy(
                src_ref=src.at[lax.div(peer, per)], dst_ref=dst.at[my], send_sem=s_sem,
                recv_sem=r_sem, device_id=(me, peer), device_id_type=MESH).start()

    def drain(ref, count, sem):
        whole = ref.at[pl.ds(0, count)]
        pltpu.make_async_copy(whole, whole, sem).wait()

    smalls[2].wait()

    def fill_msg(c):
        at, size = spans_in[c]
        piece = size // split
        total = dot(sel_t[0], tok[:, at:at + piece])
        for j in range(1, split):
            total += dot(sel_t[j], tok[:, at + j * piece:at + (j + 1) * piece])
        msg[c][...] = bf(total.reshape(nodes, SUB, piece))
        arrived[c][me] = msg[c][me]

    for c in range(n_in):
        fill_msg(c)
    pl.semaphore_wait(barrier, nodes + locals_ - 2)
    node_send(meta_out, meta_in, meta_sem.at[0], meta_sem.at[1])
    for c in range(n_in):
        node_send(msg[c], arrived[c], a_send.at[c], a_recv.at[c])

    drain(meta_in, nodes - 1, meta_sem.at[1])
    members = meta_in[...].reshape(lanes, 128)
    lane = iota((lanes, 128), 1)
    row = iota((lanes, 128), 0)
    under = bf(jnp.where(iota((lanes, lanes), 0) > iota((lanes, lanes), 1), 1.0, 0.0))
    for j in range(split):
        inside = lax.div(lax.rem(row, SUB), per_node) == j
        mine = jnp.where(inside, members, 0)
        marks = jnp.where(mine == lane + 1, 1.0, 0.0)
        before = dot(under, bf(marks))
        spot = jnp.sum(before * marks, axis=1, keepdims=True).astype(jnp.int32)
        target = jnp.where(mine > 0, (mine - 1) * cap + spot, -1)
        placed = jnp.where(lane == target, 1.0, 0.0)
        place[j] = bf(placed[:, :slots])
        pack[j] = bf(jnp.transpose(placed)[:slots, :])

    def forward(c):
        piece = spans_in[c][1] // split
        drain(arrived[c], nodes - 1, a_recv.at[c])
        got = arrived[c][...].reshape(lanes, piece)
        for j in range(split):
            bundle[c][:, :, j * piece:(j + 1) * piece] = bf(
                dot(pack[j], got).reshape(EXP_NODE, cap, piece))
        rows[c][my] = bundle[c][lax.div(my, slices)]
        local_send(bundle[c], rows[c], b_send.at[c], b_recv.at[c], slices)

    def expand(c):
        first[c][0].wait()
        first[c][1].wait()
        drain(rows[c], locals_ - 1, b_recv.at[c])
        x = rows[c][...].reshape(locals_ * cap, spans_in[c][1])
        if c == 0:
            acc_g[...] = dot(x, wg[c][...])
            acc_u[...] = dot(x, wu[c][...])
        else:
            acc_g[...] += dot(x, wg[c][...])
            acc_u[...] += dot(x, wu[c][...])

    for step in range(n_in + LAG_IN):
        if step < n_in:
            forward(step)
        if step >= LAG_IN:
            expand(step - LAG_IN)

    gate = acc_g[...]
    hidden[...] = bf(gate / (1.0 + jnp.exp(-gate)) * acc_u[...])

    def project(c):
        second[c].wait()
        part[c][...] = bf(dot(hidden[...], wd[c][...]).reshape(locals_, cap, spans_out[c][1]))
        back[c][my] = part[c][my]
        local_send(part[c], back[c], c_send.at[c], c_recv.at[c], 1)

    def relay(c):
        size = spans_out[c][1]
        piece = size // split
        drain(back[c], locals_ - 1, c_recv.at[c])
        if slices == 1:
            got = back[c][...].reshape(slots, size)
        else:
            got = bf(jnp.sum(
                back[c][...].astype(jnp.float32).reshape(EXP_NODE, slices, cap, size),
                axis=1)).reshape(slots, size)
        total = dot(place[0], got[:, 0:piece])
        for j in range(1, split):
            total += dot(place[j], got[:, j * piece:(j + 1) * piece])
        home_out[c][...] = bf(total.reshape(nodes, SUB, piece))
        home[c][me] = home_out[c][me]
        node_send(home_out[c], home[c], d_send.at[c], d_recv.at[c])

    def combine(c):
        at, size = spans_out[c]
        piece = size // split
        drain(home[c], nodes - 1, d_recv.at[c])
        got = home[c][...].reshape(lanes, piece)
        for j in range(split):
            value = dot(w_hi[j], got) + dot(w_lo[j], got)
            out_ref[:, at + j * piece:at + (j + 1) * piece] = bf(value)

    for step in range(n_out + LAG_RELAY + LAG_HOME):
        if step < n_out:
            project(step)
        if LAG_RELAY <= step < n_out + LAG_RELAY:
            relay(step - LAG_RELAY)
        if step >= LAG_RELAY + LAG_HOME:
            combine(step - LAG_RELAY - LAG_HOME)

    drain(meta_out, nodes - 1, meta_sem.at[0])
    for c in range(n_in):
        drain(msg[c], nodes - 1, a_send.at[c])
        drain(rows[c], locals_ - 1, b_send.at[c])
    for c in range(n_out):
        drain(part[c], locals_ - 1, c_send.at[c])
        drain(home_out[c], nodes - 1, d_send.at[c])


def body(tokens, expert_ids, combine_codes, gate_weight, up_weight, down_weight):
    nodes = lax.axis_size("node")
    locals_ = lax.axis_size("local")
    count, width = tokens.shape
    hid = gate_weight.shape[2]
    routes = count * TOP
    per_node = routes // nodes
    cap = min(routes, 2 * routes // EXP_NODE)
    split, spans_in, spans_out = plan(width, per_node)
    lanes = nodes * SUB
    slots = EXP_NODE * cap
    many = locals_ * cap
    b16, f32, i32 = jnp.bfloat16, jnp.float32, jnp.int32
    dims = (nodes, locals_, per_node, cap, split, spans_in, spans_out)
    dma = pltpu.SemaphoreType.DMA
    v = pltpu.VMEM
    most = max(len(spans_in), len(spans_out))
    sizes_in = [n for _, n in spans_in]
    sizes_out = [n for _, n in spans_out]
    scratch = [
        v((count, width), b16), v((TOP, count), i32), v((TOP, count), i32),
        v((nodes, SUB, 128), i32), v((nodes, SUB, 128), i32),
        v((split, lanes, count), b16), v((split, count, lanes), b16),
        v((split, count, lanes), b16),
        v((split, lanes, slots), b16), v((split, slots, lanes), b16),
        v((many, hid), f32), v((many, hid), f32), v((many, hid), b16),
        [v((n, hid), b16) for n in sizes_in],
        [v((n, hid), b16) for n in sizes_in],
        [v((nodes, SUB, n // split), b16) for n in sizes_in],
        [v((nodes, SUB, n // split), b16) for n in sizes_in],
        [v((EXP_NODE, cap, n), b16) for n in sizes_in],
        [v((locals_, cap, n), b16) for n in sizes_in],
        [v((hid, n), b16) for n in sizes_out],
        [v((locals_, cap, n), b16) for n in sizes_out],
        [v((locals_, cap, n), b16) for n in sizes_out],
        [v((nodes, SUB, n // split), b16) for n in sizes_out],
        [v((nodes, SUB, n // split), b16) for n in sizes_out],
        dma((3,)), dma((3, most)), dma((2,)),
    ] + [dma((most,)) for _ in range(8)]
    counts = [0] * 7 + [len(x) if isinstance(x, list) else 0 for x in scratch]
    flat = [y for x in scratch for y in (x if isinstance(x, list) else [x])]
    return pl.pallas_call(
        functools.partial(kernel, dims, counts),
        out_shape=pltpu.VMEM((count, width), b16),
        in_specs=[pl.BlockSpec(memory_space=pl.ANY)] * 6,
        out_specs=pl.BlockSpec(memory_space=pltpu.VMEM),
        scratch_shapes=flat,
        compiler_params=pltpu.CompilerParams(collective_id=0, has_side_effects=True),
    )(tokens, expert_ids.T, combine_codes.T, gate_weight, up_weight, down_weight)


def solution(mesh):
    in_specs = (
        P(("node", "local"), None),
        P(("node", "local"), None),
        P(("node", "local"), None),
        P(("node", "local"), None, None),
        P(("node", "local"), None, None),
        P(("node", "local"), None, None),
    )
    out_specs = P(("node", "local"), None)
    return jax.shard_map(body, mesh=mesh, in_specs=in_specs, out_specs=out_specs, check_vma=False)
```
